128 devices in a mesh: blk: 16 (over y, z), order: 8 (over x, core).
Axes of the slice: x: 4, y: 4, z: 4, core: 2. Of those that a mesh axis runs over, the one named last changes fastest.
Arguments:
- harmonics: float32 [128, 4, 8192], P('order', None, 'blk'), may hold values from -6 to 6
- legendre: float32 [128, 2, 256, 8192], P('order', None, 'blk'), may hold values from -0.005859375 to 0.005859375
- sky_map: float32 [256, 2, 16384], P(('blk', 'order')), may hold values from -6 to 6
- cycle_length: int32 [256], P(('blk', 'order')), may hold values from 4 to 16384, as said below
- cycle_offset: int32 [256], P(('blk', 'order')), may hold values from 0 to 1, as said below
- cycle_weight: float32 [256], P(('blk', 'order')), may hold values from 0.1 to 0.4
- order_ids: int32 [128], P('order'), may hold values from 0 to 8191, as said below
Outputs:
- refined: float32 [128, 4, 8192], P('order', None, 'blk')
- residual: float32 [256, 2, 16384], P(('blk', 'order'))
The draws below stay inside these ranges and needn't reach their ends.
Inputs may be any that keep to these rules, and one draw needn't show every extreme that they name: `cycle_length`: cycle lengths are multiples of 4. Of each device's 2 consecutive cycles, those at even places have 4 * 4096 pixels, those at odd places 4 j pixels for some j from 1 to 4095. `cycle_offset`: 1 on every cycle of fewer than 16384 pixels. `order_ids`: the orders are distinct; 0 and 8191 are among them. Slot s (from 0) of each index of order holds an order from s * 512 to (s + 1) * 512 - 1.
All inputs are finite; a program needn't handle non-finite values.
Results may differ from the reference program's by a relative error of at most 0.0003.
Values sent between devices are 32-bit elements; how exact they have to be, the bound alone decides.
A program may use at most 192 MiB of HBM per device.

```python
import math
import jax
import jax.numpy as jnp
from jax import lax

NSIDE = 4096
L = 8192
NPAD = 16384
M_DEV = 16
R_OWN = 2
M_TOT = 128
CYCLES = 256


def cycle_plan(key):
    position = jnp.arange(CYCLES, dtype=jnp.int32)
    within_device = position % R_OWN
    belt_cycle = NSIDE + jax.random.randint(jax.random.fold_in(key, 11), (CYCLES,), 0, 2 * NSIDE + 1)
    polar_cycle = 1 + jax.random.randint(jax.random.fold_in(key, 12), (CYCLES,), 0, NSIDE - 1)
    polar_cycle = jnp.where(position == 1, 1, polar_cycle)
    equator = within_device % 2 == 0
    length = jnp.where(equator, 4 * NSIDE, 4 * polar_cycle)
    offset = jnp.where(equator, (belt_cycle - NSIDE + 1) % 2, 1)
    return (length.astype(jnp.int32), offset.astype(jnp.int32))


def draw_cycle_length(key, part):
    return cycle_plan(key)[0]


def draw_cycle_offset(key, part):
    return cycle_plan(key)[1]


def draw_order_ids(key, part):
    stratum = L // M_DEV
    groups = M_TOT // M_DEV

    def one_slot(slot):
        picks = jax.random.permutation(jax.random.fold_in(key, 30 + slot), stratum - 2)[:groups]
        return (picks + 1 + slot * stratum).astype(jnp.int32)
    table = jax.vmap(one_slot)(jnp.arange(M_DEV, dtype=jnp.int32))
    chosen = jnp.transpose(table).reshape(M_TOT).astype(jnp.int32)
    chosen = chosen.at[0].set(0)
    chosen = chosen.at[M_TOT - 1].set(L - 1)
    return chosen


def block_levels(key, dims, cuts, low, largest):
    def one(dim, blocks):
        heights = jax.random.uniform(jax.random.fold_in(jax.random.fold_in(key, 6), dim), (blocks,), jnp.float32, low / len(cuts), largest / len(cuts))
        return jnp.repeat(jnp.exp(heights), dims[dim] // blocks).reshape((-1,) + (1,) * (len(dims) - dim - 1))

    gain = one(*cuts[0])
    for cut in cuts[1:]:
        gain = gain * one(*cut)
    return gain


def scatter_about(stream_key, shape, spread, most, split=(), kind=jnp.bfloat16):
    result = spread * jax.random.normal(stream_key, shape, jnp.float32)
    if split:
        result = result * block_levels(stream_key, shape, split, -0.22, 0.18)
    return jnp.clip(result, -most, most).astype(kind)


def setup_inputs(seed: int = 0) -> dict:
    key_of = jax.random.split(jax.random.key(seed), 8)
    harmonics = scatter_about(key_of[0], (M_TOT, 4, L), 1.0, 6.0, ((0, 8), (2, 16)), jnp.float32)
    legendre = scatter_about(key_of[1], (M_TOT, 2, CYCLES, L), (L * M_TOT) ** -0.5, 0.005859375, ((0, 8), (2, 16)), jnp.float32)
    sky_map = scatter_about(key_of[2], (CYCLES, 2, NPAD), 1.0, 6.0, ((0, 128),), jnp.float32)
    cycle_length = draw_cycle_length(jax.random.fold_in(key_of[7], 71), 0)
    cycle_offset = draw_cycle_offset(jax.random.fold_in(key_of[7], 71), 0)
    cycle_weight = jnp.clip(jnp.exp(math.log(0.4) - 1.3862944 * jax.random.uniform(key_of[5], (CYCLES,), jnp.float32) ** block_levels(key_of[5], (CYCLES,), ((0, 128),), -0.2, 0.2)), 0.1, 0.4)
    order_ids = draw_order_ids(jax.random.fold_in(key_of[7], 71), 0)
    return {"harmonics": harmonics, "legendre": legendre, "sky_map": sky_map, "cycle_length": cycle_length, "cycle_offset": cycle_offset, "cycle_weight": cycle_weight, "order_ids": order_ids}


HIGHEST = lax.Precision.HIGHEST

def cycle_tables(orders, length, offset, first_pixel, block_width):
    pixels = first_pixel + lax.iota(jnp.int32, block_width)
    phase_turns = orders[:, None] * (2 * pixels + offset)[None, :] % (2 * length)
    angles = phase_turns.astype(jnp.float32) * (math.pi / length.astype(jnp.float32))
    inside = (pixels < length).astype(jnp.float32)
    return (jnp.concatenate([jnp.cos(angles), jnp.sin(angles)], axis=0), inside)

def synth_weights(phases, factor):
    scaled = phases * factor[:, None]
    first_row = jnp.concatenate([scaled[:, 0], -scaled[:, 1]])
    second_row = jnp.concatenate([scaled[:, 2], -scaled[:, 3]])
    return jnp.stack([first_row, second_row])

def fold_totals(totals, weighting):
    half = totals.shape[1] // 2
    return weighting * jnp.stack([totals[0, :half], -totals[0, half:], totals[1, :half], -totals[1, half:]], axis=1)

def assemble(products):
    positive = products[:, 0]
    negative = products[:, 1]
    return jnp.stack([-positive[:, 0] + negative[:, 3], -positive[:, 1] - negative[:, 2], -positive[:, 2] - negative[:, 1], -positive[:, 3] + negative[:, 0]], axis=1)

def adjoint_coeffs(returned):
    positive = -returned
    negative = jnp.stack([returned[:, 3], -returned[:, 2], -returned[:, 1], returned[:, 0]], axis=1)
    return jnp.stack([positive, negative], axis=1)

def reference(harmonics, legendre, sky_map, cycle_length, cycle_offset, cycle_weight, order_ids):
    degrees = jnp.arange(L, dtype=jnp.int32)
    valid_mask = (degrees[None, :] >= jnp.maximum(order_ids, 2)[:, None]).astype(jnp.float32)
    coefficients = harmonics * valid_mask[:, None, :]

    def forward(operands):
        tables, values = operands
        return jnp.einsum('trl,cl->tcr', tables, values, precision=HIGHEST)
    products = lax.map(forward, (legendre, coefficients))
    phases = assemble(products)
    factor = jnp.where(order_ids == 0, 1.0, 2.0).astype(jnp.float32)
    normalise = math.sqrt(L * M_TOT / (CYCLES * NPAD))

    def per_cycle(inputs):
        cycle_phases, sky_row, length, offset, weight = inputs
        weights = synth_weights(cycle_phases, factor)
        trig_table, inside = cycle_tables(order_ids, length, offset, 0, NPAD)
        modelled = jnp.dot(weights, trig_table, precision=HIGHEST)
        residual = (sky_row - modelled) * inside[None, :]
        totals = lax.dot_general(residual, trig_table, (((1,), (1,)), ((), ())), precision=HIGHEST)
        return (residual, fold_totals(totals, weight * normalise))
    residual, analysed = lax.map(per_cycle, (jnp.transpose(phases, (2, 0, 1)), sky_map, cycle_length, cycle_offset, cycle_weight))
    coeffs = adjoint_coeffs(jnp.transpose(analysed, (1, 2, 0)))

    def backward(operands):
        tables, weights = operands
        return jnp.einsum('trl,tar->al', tables, weights, precision=HIGHEST)
    update = lax.map(backward, (legendre, coeffs))
    refined = valid_mask[:, None, :] * (harmonics + update)
    return (refined, residual)
```

```python
import functools
import math

import jax
import jax.numpy as jnp
from jax import lax
from jax.experimental import pallas as pl
from jax.experimental.pallas import tpu as pltpu
from jax.sharding import PartitionSpec as P

HIGHEST = lax.Precision.HIGHEST
F32 = jnp.float32
SLOTS = 16
BLOCKS = 16
WIDTH = 512
GROUP = 8
LANES = 128
VMEM_LIMIT = 60 * 1024 * 1024


def lane_iota(shape):
    return lax.broadcasted_iota(jnp.int32, shape, len(shape) - 1)


def row_iota(shape):
    return lax.broadcasted_iota(jnp.int32, shape, 0)


def table_copies(leg_ref, tables, sems):
    copies = []
    for s in range(SLOTS):
        cut = pl.ds(s * WIDTH, (BLOCKS - s) * WIDTH)
        copies.append(
            pltpu.make_async_copy(
                leg_ref.at[s, :, :, cut], tables.at[s, :, :, cut], sems.at[s]
            )
        )
    return copies


def forward_column(accs, tables, gathered, s, b, j, keep=None):
    lanes = pl.ds(pl.multiple_of(b * WIDTH + j * LANES, LANES), LANES)
    values = [
        jnp.broadcast_to(gathered[b, s, a : a + 1, j * LANES : (j + 1) * LANES], (8, LANES))
        for a in range(4)
    ]
    if keep is not None:
        values = [jnp.where(keep, v, 0.0) for v in values]
    out = []
    for half in range(2):
        plus = tables[s, 0, half * 8 : half * 8 + 8, lanes]
        minus = tables[s, 1, half * 8 : half * 8 + 8, lanes]
        a0, a1, a2, a3 = accs[half * 4 : half * 4 + 4]
        out += [
            a0 + (minus * values[3] - plus * values[0]),
            a1 - (plus * values[1] + minus * values[2]),
            a2 - (plus * values[2] + minus * values[1]),
            a3 + (minus * values[0] - plus * values[3]),
        ]
    return tuple(out)


def forward_slot(tables, gathered, floor, s):
    accs = tuple(jnp.zeros((8, LANES), F32) for _ in range(8))
    for j in range(WIDTH // LANES):
        degrees = s * WIDTH + j * LANES + lane_iota((8, LANES))
        accs = forward_column(accs, tables, gathered, s, s, j, degrees >= floor)

    def step(b, accs):
        for j in range(WIDTH // LANES):
            accs = forward_column(accs, tables, gathered, s, b, j)
        return accs

    return lax.fori_loop(s + 1, BLOCKS, step, accs)


def forward_kernel(ids_ref, leg_ref, gathered, out_ref, tables, sems):
    copies = table_copies(leg_ref, tables, sems)
    for copy in reversed(copies):
        copy.start()
    slot_of_lane = lane_iota((8, LANES)) % SLOTS
    sums = [jnp.zeros((8, LANES), F32) for _ in range(8)]
    orders = jnp.zeros((8, LANES), F32)
    for s in reversed(range(SLOTS)):
        here = slot_of_lane == s
        orders = jnp.where(here, ids_ref[s].astype(F32), orders)
        copies[s].wait()
        accs = forward_slot(tables, gathered, jnp.maximum(ids_ref[s], 2), s)
        for i in range(8):
            sums[i] = jnp.where(here, jnp.sum(accs[i], axis=1, keepdims=True), sums[i])
    zero = jnp.zeros((8, LANES), F32)
    for half in range(2):
        rows = sums[half * 4 : half * 4 + 4] + [orders, zero, zero, zero]
        for a in range(8):
            out_ref[pl.ds(half * 64 + a, 8, stride=8), :] = rows[a]


def forward(order_ids, legendre, gathered):
    return pl.pallas_call(
        forward_kernel,
        out_shape=jax.ShapeDtypeStruct((128, LANES), F32),
        in_specs=[
            pl.BlockSpec(memory_space=pltpu.SMEM),
            pl.BlockSpec(memory_space=pl.ANY),
            pl.BlockSpec(memory_space=pltpu.VMEM),
        ],
        out_specs=pl.BlockSpec(memory_space=pltpu.VMEM),
        scratch_shapes=[
            pltpu.VMEM(legendre.shape, F32),
            pltpu.SemaphoreType.DMA((SLOTS,)),
        ],
        compiler_params=pltpu.CompilerParams(vmem_limit_bytes=VMEM_LIMIT),
        name="forward",
    )(order_ids, legendre, gathered)


def turn_tables(n, quarter_rate, half_length, unit):
    turns = jnp.floor(n * quarter_rate + 0.5)
    x = (n - turns * half_length) * unit
    q = turns.astype(jnp.int32) & 3
    z = x * x
    sin = ((-1.9515295891e-4 * z + 8.3321608736e-3) * z - 1.6666654611e-1) * z * x + x
    cos = (
        (2.443315711809948e-5 * z - 1.388731625493765e-3) * z + 4.166664568298827e-2
    ) * z * z - 0.5 * z + 1.0
    odd = (q & 1) == 1
    c = jnp.where(odd, sin, cos)
    s = jnp.where(odd, cos, sin)
    c = jnp.where((q == 1) | (q == 2), -c, c)
    s = jnp.where(q >= 2, -s, s)
    return c, s


def wrap(n, period):
    rest = n - jnp.floor(n / period) * period
    rest = jnp.where(rest < 0.0, rest + period, rest)
    return jnp.where(rest >= period, rest - period, rest)


def cycle_setup(orders, length, offset):
    length_row = jnp.full((1, LANES), length.astype(F32))
    period = 2.0 * length_row
    half_length = 0.5 * length_row
    quarter_rate = 2.0 / length_row
    unit = math.pi / length_row
    low = wrap(orders, period)
    high = wrap(low * 256.0, period)
    shape = (256, LANES)
    kh = (row_iota(shape) // 2).astype(F32)
    kl = (2 * row_iota((LANES, LANES)) + offset).astype(F32)
    cos_a, sin_a = turn_tables(high * kh, quarter_rate, half_length, unit)
    cos_b, sin_b = turn_tables(low * kl, quarter_rate, half_length, unit)
    return cos_a, sin_a, jnp.concatenate([cos_b, sin_b], axis=1)


def cycle_phase(block, sky, length, offset, weight):
    orders = block[4:5, :]
    cos_a, sin_a, table = cycle_setup(orders, length, offset)
    factor = jnp.where(orders == 0.0, 1.0, 2.0)
    scaled = block * factor
    shape = (256, LANES)
    rows = row_iota(shape)
    first = (rows & 1) == 0
    real = jnp.where(first, scaled[0:1, :], scaled[2:3, :])
    imag = jnp.where(first, scaled[1:2, :], scaled[3:4, :])
    left = jnp.concatenate(
        [real * cos_a - imag * sin_a, -(real * sin_a + imag * cos_a)], axis=1
    )
    model = lax.dot_general(
        left, table, (((1,), (1,)), ((), ())), precision=HIGHEST, preferred_element_type=F32
    )
    pixels = (rows // 2) * LANES + lane_iota(shape)
    residual = jnp.where(pixels < length, sky - model, 0.0)
    totals = lax.dot_general(
        residual, table, (((1,), (0,)), ((), ())), precision=HIGHEST, preferred_element_type=F32
    )
    tc, ts = totals[:, :LANES], totals[:, LANES:]
    cos_sum = jnp.sum((cos_a * tc - sin_a * ts).reshape(32, 8, LANES), axis=0)
    sin_sum = jnp.sum((sin_a * tc + cos_a * ts).reshape(32, 8, LANES), axis=0)
    out = []
    for part in (cos_sum, sin_sum):
        part = part + pltpu.roll(part, 2, 0)
        out.append(part + pltpu.roll(part, 4, 0))
    cos_sum, sin_sum = out
    rows = row_iota((8, LANES))
    analysed = jnp.where(
        rows == 0,
        cos_sum[0:1, :],
        jnp.where(
            rows == 1,
            -sin_sum[0:1, :],
            jnp.where(rows == 2, cos_sum[1:2, :], jnp.where(rows == 3, -sin_sum[1:2, :], 0.0)),
        ),
    )
    return residual, analysed * weight


def pixel_kernel(scale, length, offset, weight, phases, sky, residual_ref, out_ref):
    owner = lane_iota((8, LANES)) // SLOTS
    for c in range(2):
        block = jnp.zeros((8, LANES), F32)
        for o in range(GROUP):
            piece = phases[o * 16 + c * 8 : o * 16 + c * 8 + 8, :]
            block = jnp.where(owner == o, piece, block)
        residual, analysed = cycle_phase(
            block, sky[c], length[c], offset[c], weight[c] * scale
        )
        residual_ref[c] = residual
        for o in range(GROUP):
            out_ref[o * 16 + c * 8 : o * 16 + c * 8 + 8, :] = analysed


def pixel_phase(scale, length, offset, weight, phases, sky):
    smem = pl.BlockSpec(memory_space=pltpu.SMEM)
    vmem = pl.BlockSpec(memory_space=pltpu.VMEM)
    return pl.pallas_call(
        functools.partial(pixel_kernel, scale),
        out_shape=(
            jax.ShapeDtypeStruct(sky.shape, F32),
            jax.ShapeDtypeStruct((128, LANES), F32),
        ),
        in_specs=[smem, smem, smem, vmem, vmem],
        out_specs=(vmem, vmem),
        name="pixel_phase",
    )(length, offset, weight, phases, sky)


def merge_rows(x, y, shift, bit):
    return jnp.where(bit, y, x) + pltpu.roll(jnp.where(bit, x, y), shift, 0)


def adjoint_tile(tables, weights, s, b, store):
    rows = row_iota((8, LANES))
    bits = [(rows & n) != 0 for n in (1, 2, 4)]
    for pair in range(WIDTH // LANES // 2):
        parts = []
        for j in (2 * pair, 2 * pair + 1):
            lanes = pl.ds(pl.multiple_of(b * WIDTH + j * LANES, LANES), LANES)
            sums = [None] * 4
            for half in range(2):
                plus = tables[s, 0, half * 8 : half * 8 + 8, lanes]
                minus = tables[s, 1, half * 8 : half * 8 + 8, lanes]
                w = weights[half * 4 : half * 4 + 4]
                terms = [
                    minus * w[3] - plus * w[0],
                    -(plus * w[1] + minus * w[2]),
                    -(plus * w[2] + minus * w[1]),
                    minus * w[0] - plus * w[3],
                ]
                sums = [t if x is None else x + t for x, t in zip(sums, terms)]
            parts += sums
        for level, shift in enumerate((1, 2, 4)):
            parts = [
                merge_rows(parts[2 * i], parts[2 * i + 1], shift, bits[level])
                for i in range(len(parts) // 2)
            ]
        store(pair, parts[0])


def slot_weights(columns, s):
    return [jnp.broadcast_to(c[:, s : s + 1], (8, LANES)) for c in columns]


def own_columns(returned, me):
    columns = []
    shift = (LANES - SLOTS * me) % LANES
    for half in range(2):
        for a in range(4):
            rows = returned[pl.ds(half * 64 + a, 8, stride=8), :]
            columns.append(pltpu.roll(rows, shift, 1))
    return columns


def adjoint_kernel(leg_ref, returned, out_ref, tables, sems):
    copies = table_copies(leg_ref, tables, sems)
    for copy in reversed(copies):
        copy.start()
    columns = own_columns(returned, lax.axis_index("order"))
    for s in reversed(range(SLOTS)):
        weights = slot_weights(columns, s)
        copies[s].wait()

        def clear(b, carry):
            out_ref[b, s] = jnp.zeros((4, WIDTH), F32)
            return carry

        def step(b, carry):
            def store(pair, block):
                out_ref[b, s, :, pair * 256 : pair * 256 + 128] = block[0:4]
                out_ref[b, s, :, pair * 256 + 128 : pair * 256 + 256] = block[4:8]

            adjoint_tile(tables, weights, s, b, store)
            return carry

        lax.fori_loop(0, s, clear, 0)
        lax.fori_loop(s, BLOCKS, step, 0)


def adjoint(legendre, returned):
    return pl.pallas_call(
        adjoint_kernel,
        out_shape=jax.ShapeDtypeStruct((BLOCKS, SLOTS, 4, WIDTH), F32),
        in_specs=[
            pl.BlockSpec(memory_space=pl.ANY),
            pl.BlockSpec(memory_space=pltpu.VMEM),
        ],
        out_specs=pl.BlockSpec(memory_space=pltpu.VMEM),
        scratch_shapes=[
            pltpu.VMEM(legendre.shape, F32),
            pltpu.SemaphoreType.DMA((SLOTS,)),
        ],
        compiler_params=pltpu.CompilerParams(vmem_limit_bytes=VMEM_LIMIT),
        name="adjoint",
    )(legendre, returned)


def to_rows(sky):
    cycles = sky.shape[0]
    parts = sky.reshape(cycles, 2, LANES, LANES)
    return jnp.transpose(parts, (0, 2, 1, 3)).reshape(cycles, 2 * LANES, LANES)


def from_rows(rows):
    cycles = rows.shape[0]
    parts = rows.reshape(cycles, LANES, 2, LANES)
    return jnp.transpose(parts, (0, 2, 1, 3)).reshape(cycles, 2, LANES * LANES)


def body(harmonics, legendre, sky_map, cycle_length, cycle_offset, cycle_weight, order_ids):
    scale = math.sqrt(8192 * 128 / 4194304)
    gathered = lax.all_gather(harmonics, "blk", axis=0)
    message = forward(order_ids, legendre, gathered)
    phases = lax.all_to_all(
        message.reshape(GROUP, 16, LANES), "order", split_axis=0, concat_axis=0
    ).reshape(128, LANES)
    rows, message = pixel_phase(
        scale, cycle_length, cycle_offset, cycle_weight, phases, to_rows(sky_map)
    )
    returned = lax.all_to_all(
        message.reshape(GROUP, 16, LANES), "order", split_axis=0, concat_axis=0
    ).reshape(128, LANES)
    update = adjoint(legendre, returned)
    own_update = lax.psum_scatter(update, "blk", scatter_dimension=0)
    degrees = lax.axis_index("blk") * WIDTH + lax.iota(jnp.int32, WIDTH)
    floors = jnp.maximum(order_ids, 2)
    mask = (degrees[None, :] >= floors[:, None])[:, None, :]
    refined = jnp.where(mask, harmonics + own_update, 0.0)
    return refined, from_rows(rows)


def solution(mesh):
    return jax.shard_map(
        body,
        mesh=mesh,
        in_specs=(
            P("order", None, "blk"),
            P("order", None, "blk", None),
            P(("blk", "order"), None, None),
            P(("blk", "order")),
            P(("blk", "order")),
            P(("blk", "order")),
            P("order"),
        ),
        out_specs=(P("order", None, "blk"), P(("blk", "order"), None, None)),
        check_vma=False,
    )
```

```python
import functools
import math

import jax
import jax.numpy as jnp
from jax import lax
from jax.experimental import pallas as pl
from jax.experimental.pallas import tpu as pltpu
from jax.sharding import PartitionSpec as P

HIGHEST = lax.Precision.HIGHEST
F32 = jnp.float32
SLOTS = 16
BLOCKS = 16
WIDTH = 512
GROUP = 8
LANES = 128
HALF = WIDTH // 2
VMEM_LIMIT = 60 * 1024 * 1024


def lane_iota(shape):
    return lax.broadcasted_iota(jnp.int32, shape, len(shape) - 1)


def row_iota(shape):
    return lax.broadcasted_iota(jnp.int32, shape, 0)


def slot_pairs(b):
    return (b + 2) // 2


def table_copies(leg_ref, tables, sems):
    copies = []
    for s in range(SLOTS):
        cut = pl.ds(s // 2 * 2 * WIDTH, (BLOCKS - s // 2 * 2) * WIDTH)
        copies.append(
            pltpu.make_async_copy(
                leg_ref.at[s, :, :, cut], tables.at[s, :, :, cut], sems.at[s]
            )
        )
    return copies


LEGS = [(0, 0, d, relay) for relay in (0, 1) for d in (1, -1)]
LEGS += [(1, f, d, relay) for f in (0, 1, -1, 2) for relay in (0, 1) for d in (1, -1)]
LEG_INDEX = {leg: k for k, leg in enumerate(LEGS)}


class Routes:
    def __init__(self):
        blk = lax.axis_index("blk")
        self.y, self.z = blk // 4, blk % 4
        self.me = blk

    def block(self, h, f, s):
        dy, dz = (f, s) if h == 0 else (s, f)
        return (self.y + dy + 8) % 4 * 4 + (self.z + dz + 8) % 4

    def neighbour(self, h, leg, sign):
        axis, _, d, _ = leg
        return self.block(h, sign * d, 0) if axis == 0 else self.block(h, 0, sign * d)

    def sent(self, h, leg):
        axis, f, d, relay = leg
        back = -d if relay else 0
        return self.block(h, back, 0) if axis == 0 else self.block(h, f, back)

    def received(self, h, leg):
        axis, f, d, relay = leg
        back = -2 * d if relay else -d
        return self.block(h, back, 0) if axis == 0 else self.block(h, f, back)

    def neighbours(self):
        return [self.block(0, 1, 0), self.block(0, -1, 0), self.block(0, 0, 1), self.block(0, 0, -1)]


CUTS = 4


def leg_cuts(b):
    return b // 4 + 1


def leg_cut(leg, b, c):
    _, _, d, relay = leg
    size = 2 if relay else 4
    first = 2 * leg_cuts(b) if relay and d == -1 else 0
    return pl.ds(first + c * size, size)


def each_cut(b, act):
    def step(c, carry):
        act(c)
        return carry

    lax.fori_loop(0, leg_cuts(b), step, 0)


def greet(axis, partners):
    barrier = pltpu.get_barrier_semaphore()
    for partner in partners:
        pl.semaphore_signal(barrier, 1, device_id={axis: partner})
    pl.semaphore_wait(barrier, len(partners))


def forward_pair(acc, tables, gathered, ids_ref, b, i, masked):
    for s in (2 * i, 2 * i + 1):
        accs = [acc[s, q] for q in range(8)]
        for j in range(WIDTH // LANES):
            lanes = pl.ds(pl.multiple_of(b * WIDTH + j * LANES, LANES), LANES)
            h, at = j // 2, j % 2 * LANES
            values = [
                jnp.broadcast_to(gathered[h, b, s, a : a + 1, at : at + LANES], (8, LANES))
                for a in range(4)
            ]
            if masked:
                degrees = b * WIDTH + j * LANES + lane_iota((8, LANES))
                keep = degrees >= jnp.maximum(ids_ref[s], 2)
                values = [jnp.where(keep, v, 0.0) for v in values]
            for r in range(2):
                plus = tables[s, 0, r * 8 : r * 8 + 8, lanes]
                minus = tables[s, 1, r * 8 : r * 8 + 8, lanes]
                a0, a1, a2, a3 = accs[r * 4 : r * 4 + 4]
                accs[r * 4 : r * 4 + 4] = [
                    a0 + (minus * values[3] - plus * values[0]),
                    a1 - (plus * values[1] + minus * values[2]),
                    a2 - (plus * values[2] + minus * values[1]),
                    a3 + (minus * values[0] - plus * values[3]),
                ]
        for q in range(8):
            acc[s, q] = accs[q]


def forward_block(acc, tables, gathered, ids_ref, b):
    last = slot_pairs(b) - 1

    def step(i, carry):
        forward_pair(acc, tables, gathered, ids_ref, b, i, False)
        return carry

    lax.fori_loop(0, last, step, 0)
    forward_pair(acc, tables, gathered, ids_ref, b, last, True)


def write_message(acc, ids_ref, out_ref):
    slot_of_lane = lane_iota((8, LANES)) % SLOTS
    sums = [jnp.zeros((8, LANES), F32) for _ in range(8)]
    orders = jnp.zeros((8, LANES), F32)
    for s in range(SLOTS):
        here = slot_of_lane == s
        orders = jnp.where(here, ids_ref[s].astype(F32), orders)
        for q in range(8):
            sums[q] = jnp.where(here, jnp.sum(acc[s, q], axis=1, keepdims=True), sums[q])
    zero = jnp.zeros((8, LANES), F32)
    for r in range(2):
        rows = sums[r * 4 : r * 4 + 4] + [orders, zero, zero, zero]
        for a in range(8):
            for i in range(8):
                at = r * 64 + i * 8 + a
                out_ref[at : at + 1, :] = rows[a][i : i + 1, :]


def gather_forward_kernel(
    ids_ref, leg_ref, harm_ref, out_ref, tables, gathered, acc,
    table_sems, own_sems, send_sems, recv_sems,
):
    routes = Routes()
    loads = table_copies(leg_ref, tables, table_sems)
    own = [
        pltpu.make_async_copy(
            harm_ref.at[:, :, pl.ds(h * HALF, HALF)], gathered.at[h, routes.me], own_sems.at[h]
        )
        for h in range(2)
    ]
    greet("blk", routes.neighbours())

    def copy(h, leg, b, target, c):
        cut = leg_cut(leg, b, c)
        k = (h * len(LEGS) + LEG_INDEX[leg]) * CUTS + c
        axis, f, d, relay = leg
        source = gathered.at[h, b, cut]
        if f == 0 and not relay:
            source = harm_ref.at[cut, :, pl.ds(h * HALF, HALF)]
        return pltpu.make_async_remote_copy(
            src_ref=source,
            dst_ref=gathered.at[h, b, cut],
            send_sem=send_sems.at[k],
            recv_sem=recv_sems.at[k],
            device_id={"blk": target},
        )

    started = []

    def send(*leg):
        for h in range(2):
            for d in (1, -1):
                full = (leg[0], leg[1], d, leg[2])
                b, target = routes.sent(h, full), routes.neighbour(h, full, 1)
                each_cut(b, lambda c: copy(h, full, b, target, c).start())
                started.append((h, full, b, target))

    def arrive(*leg):
        for h in range(2):
            for d in (1, -1):
                full = (leg[0], leg[1], d, leg[2])
                b, target = routes.received(h, full), routes.neighbour(h, full, 1)
                each_cut(b, lambda c: copy(h, full, b, target, c).wait_recv())

    def compute(places):
        for dy, dz in places:
            forward_block(acc, tables, gathered, ids_ref, routes.block(0, dy, dz))

    send(0, 0, 0)
    send(1, 0, 0)
    for c in own + loads[::-1]:
        c.start()
    for s in range(SLOTS):
        for q in range(8):
            acc[s, q] = jnp.zeros((8, LANES), F32)
    arrive(0, 0, 0)
    send(1, 1, 0)
    send(1, -1, 0)
    send(0, 0, 1)
    arrive(1, 0, 0)
    send(1, 0, 1)
    for c in own + loads[::-1]:
        c.wait()
    compute([(0, 0), (1, 0), (-1, 0)])
    arrive(0, 0, 1)
    send(1, 2, 0)
    arrive(1, 1, 0)
    send(1, 1, 1)
    arrive(1, -1, 0)
    send(1, -1, 1)
    arrive(1, 0, 1)
    compute([(0, 1), (0, -1), (1, 1), (1, -1), (-1, 1), (-1, -1)])
    arrive(1, 2, 0)
    send(1, 2, 1)
    compute([(2, 0), (0, 2)])
    arrive(1, 1, 1)
    arrive(1, -1, 1)
    compute([(2, 1), (2, -1), (1, 2), (-1, 2)])
    arrive(1, 2, 1)
    compute([(2, 2)])
    write_message(acc, ids_ref, out_ref)
    for h, full, b, target in started:
        each_cut(b, lambda c: copy(h, full, b, target, c).wait_send())


def gather_forward(order_ids, legendre, harmonics):
    legs = 2 * len(LEGS)
    return pl.pallas_call(
        gather_forward_kernel,
        out_shape=jax.ShapeDtypeStruct((128, LANES), F32),
        in_specs=[
            pl.BlockSpec(memory_space=pltpu.SMEM),
            pl.BlockSpec(memory_space=pl.ANY),
            pl.BlockSpec(memory_space=pl.ANY),
        ],
        out_specs=pl.BlockSpec(memory_space=pltpu.VMEM),
        scratch_shapes=[
            pltpu.VMEM(legendre.shape, F32),
            pltpu.VMEM((2, BLOCKS, SLOTS, 4, HALF), F32),
            pltpu.VMEM((SLOTS, 8, 8, LANES), F32),
            pltpu.SemaphoreType.DMA((SLOTS,)),
            pltpu.SemaphoreType.DMA((2,)),
            pltpu.SemaphoreType.DMA((legs * CUTS,)),
            pltpu.SemaphoreType.DMA((legs * CUTS,)),
        ],
        compiler_params=pltpu.CompilerParams(
            collective_id=0, has_side_effects=True, vmem_limit_bytes=VMEM_LIMIT
        ),
        name="gather_forward",
    )(order_ids, legendre, harmonics)


def turn_tables(n, quarter_rate, half_length, unit):
    turns = jnp.floor(n * quarter_rate + 0.5)
    x = (n - turns * half_length) * unit
    q = turns.astype(jnp.int32) & 3
    z = x * x
    sin = ((-1.9515295891e-4 * z + 8.3321608736e-3) * z - 1.6666654611e-1) * z * x + x
    cos = (
        (2.443315711809948e-5 * z - 1.388731625493765e-3) * z + 4.166664568298827e-2
    ) * z * z - 0.5 * z + 1.0
    odd = (q & 1) == 1
    c = jnp.where(odd, sin, cos)
    s = jnp.where(odd, cos, sin)
    c = jnp.where((q == 1) | (q == 2), -c, c)
    s = jnp.where(q >= 2, -s, s)
    return c, s


def wrap(n, period):
    rest = n - jnp.floor(n / period) * period
    rest = jnp.where(rest < 0.0, rest + period, rest)
    return jnp.where(rest >= period, rest - period, rest)


def cycle_setup(orders, length, offset):
    length_row = jnp.full((1, LANES), length.astype(F32))
    period = 2.0 * length_row
    half_length = 0.5 * length_row
    quarter_rate = 2.0 / length_row
    unit = math.pi / length_row
    low = wrap(orders, period)
    high = wrap(low * 256.0, period)
    shape = (256, LANES)
    kh = (row_iota(shape) // 2).astype(F32)
    kl = (2 * row_iota((LANES, LANES)) + offset).astype(F32)
    cos_a, sin_a = turn_tables(high * kh, quarter_rate, half_length, unit)
    cos_b, sin_b = turn_tables(low * kl, quarter_rate, half_length, unit)
    return cos_a, sin_a, jnp.concatenate([cos_b, sin_b], axis=1)


def cycle_phase(block, sky, length, offset, weight):
    orders = block[4:5, :]
    cos_a, sin_a, table = cycle_setup(orders, length, offset)
    factor = jnp.where(orders == 0.0, 1.0, 2.0)
    scaled = block * factor
    shape = (256, LANES)
    rows = row_iota(shape)
    first = (rows & 1) == 0
    real = jnp.where(first, scaled[0:1, :], scaled[2:3, :])
    imag = jnp.where(first, scaled[1:2, :], scaled[3:4, :])
    left = jnp.concatenate(
        [real * cos_a - imag * sin_a, -(real * sin_a + imag * cos_a)], axis=1
    )
    model = lax.dot_general(
        left, table, (((1,), (1,)), ((), ())), precision=HIGHEST, preferred_element_type=F32
    )
    pixels = (rows // 2) * LANES + lane_iota(shape)
    residual = jnp.where(pixels < length, sky - model, 0.0)
    totals = lax.dot_general(
        residual, table, (((1,), (0,)), ((), ())), precision=HIGHEST, preferred_element_type=F32
    )
    tc, ts = totals[:, :LANES], totals[:, LANES:]
    cos_sum = jnp.sum((cos_a * tc - sin_a * ts).reshape(32, 8, LANES), axis=0)
    sin_sum = jnp.sum((sin_a * tc + cos_a * ts).reshape(32, 8, LANES), axis=0)
    out = []
    for part in (cos_sum, sin_sum):
        part = part + pltpu.roll(part, 2, 0)
        out.append(part + pltpu.roll(part, 4, 0))
    cos_sum, sin_sum = out
    rows = row_iota((8, LANES))
    analysed = jnp.where(
        rows == 0,
        cos_sum[0:1, :],
        jnp.where(
            rows == 1,
            -sin_sum[0:1, :],
            jnp.where(rows == 2, cos_sum[1:2, :], jnp.where(rows == 3, -sin_sum[1:2, :], 0.0)),
        ),
    )
    return residual, analysed * weight


def pixel_kernel(
    scale, length, offset, weight, message, sky, residual_ref, returned,
    phases, reply, send_sems, recv_sems,
):
    me = lax.axis_index("order")
    greet("order", [(me + d) % GROUP for d in range(1, GROUP)])

    def rows_of(o):
        return pl.ds(pl.multiple_of(o * 16, 16), 16)

    def copies(way, source, target):
        out = []
        for d in range(1, GROUP):
            k = way * GROUP + d
            out.append(
                pltpu.make_async_remote_copy(
                    src_ref=source((me + d) % GROUP),
                    dst_ref=target.at[rows_of(me)],
                    send_sem=send_sems.at[k],
                    recv_sem=recv_sems.at[k],
                    device_id={"order": (me + d) % GROUP},
                )
            )
        return out

    out = copies(0, lambda o: message.at[rows_of(o)], phases)
    for c in out:
        c.start()
    phases[rows_of(me), :] = message[rows_of(me), :]
    for c in out:
        c.wait_recv()
    owner = lane_iota((8, LANES)) // SLOTS
    for c in range(2):
        block = jnp.zeros((8, LANES), F32)
        for o in range(GROUP):
            piece = phases[o * 16 + c * 8 : o * 16 + c * 8 + 8, :]
            block = jnp.where(owner == o, piece, block)
        residual, analysed = cycle_phase(
            block, sky[c], length[c], offset[c], weight[c] * scale
        )
        residual_ref[c] = residual
        reply[c * 8 : c * 8 + 8, :] = analysed
    back = copies(1, lambda o: reply, returned)
    for c in back:
        c.start()
    returned[rows_of(me), :] = reply[...]
    for c in back:
        c.wait_recv()
    for c in out + back:
        c.wait_send()


def pixel_phase(scale, length, offset, weight, message, sky):
    smem = pl.BlockSpec(memory_space=pltpu.SMEM)
    vmem = pl.BlockSpec(memory_space=pltpu.VMEM)
    return pl.pallas_call(
        functools.partial(pixel_kernel, scale),
        out_shape=(
            jax.ShapeDtypeStruct(sky.shape, F32),
            jax.ShapeDtypeStruct((128, LANES), F32),
        ),
        in_specs=[smem, smem, smem, vmem, vmem],
        out_specs=(vmem, vmem),
        scratch_shapes=[
            pltpu.VMEM((128, LANES), F32),
            pltpu.VMEM((16, LANES), F32),
            pltpu.SemaphoreType.DMA((2 * GROUP,)),
            pltpu.SemaphoreType.DMA((2 * GROUP,)),
        ],
        compiler_params=pltpu.CompilerParams(collective_id=1, has_side_effects=True),
        name="pixel_phase",
    )(length, offset, weight, message, sky)


def merge_rows(x, y, shift, bit):
    return jnp.where(bit, y, x) + pltpu.roll(jnp.where(bit, x, y), shift, 0)


def adjoint_pair(update, tables, weights, bits, b, i):
    for s in (2 * i, 2 * i + 1):
        w = [weights[s, q] for q in range(8)]
        for h in range(2):
            parts = []
            for j in (2 * h, 2 * h + 1):
                lanes = pl.ds(pl.multiple_of(b * WIDTH + j * LANES, LANES), LANES)
                sums = [None] * 4
                for r in range(2):
                    plus = tables[s, 0, r * 8 : r * 8 + 8, lanes]
                    minus = tables[s, 1, r * 8 : r * 8 + 8, lanes]
                    w0, w1, w2, w3 = w[r * 4 : r * 4 + 4]
                    terms = [
                        minus * w3 - plus * w0,
                        -(plus * w1 + minus * w2),
                        -(plus * w2 + minus * w1),
                        minus * w0 - plus * w3,
                    ]
                    sums = [t if x is None else x + t for x, t in zip(sums, terms)]
                parts += sums
            for level, shift in enumerate((1, 2, 4)):
                parts = [
                    merge_rows(parts[2 * n], parts[2 * n + 1], shift, bits[level])
                    for n in range(len(parts) // 2)
                ]
            update[h, b, s, :, 0:LANES] = parts[0][0:4]
            update[h, b, s, :, LANES : 2 * LANES] = parts[0][4:8]


def adjoint_block(update, tables, weights, b):
    rows = row_iota((8, LANES))
    bits = [(rows & n) != 0 for n in (1, 2, 4)]

    def step(i, carry):
        adjoint_pair(update, tables, weights, bits, b, i)
        return carry

    lax.fori_loop(0, slot_pairs(b), step, 0)


def write_weights(returned, weights, me):
    shift = (LANES - SLOTS * me) % LANES
    for r in range(2):
        for a in range(4):
            lines = [r * 64 + i * 8 + a for i in range(8)]
            rows = jnp.concatenate([returned[n : n + 1, :] for n in lines], axis=0)
            rows = pltpu.roll(rows, shift, 1)
            for s in range(SLOTS):
                weights[s, r * 4 + a] = jnp.broadcast_to(rows[:, s : s + 1], (8, LANES))


def adjoint_scatter_kernel(
    ids_ref, leg_ref, harm_ref, returned, refined, tables, update, landed, weights,
    table_sems, send_sems, recv_sems,
):
    routes = Routes()
    loads = table_copies(leg_ref, tables, table_sems)
    for c in loads[::-1]:
        c.start()
    greet("blk", routes.neighbours())
    write_weights(returned, weights, lax.axis_index("order"))
    for c in loads[::-1]:
        c.wait()

    def copy(h, leg, b, target, c):
        cut = leg_cut(leg, b, c)
        leg_id = h * len(LEGS) + LEG_INDEX[leg]
        k = leg_id * CUTS + c
        return pltpu.make_async_remote_copy(
            src_ref=update.at[h, b, cut],
            dst_ref=landed.at[leg_id, cut],
            send_sem=send_sems.at[k],
            recv_sem=recv_sems.at[k],
            device_id={"blk": target},
        )

    started = []

    def send(*leg):
        for h in range(2):
            for d in (1, -1):
                full = (leg[0], leg[1], d, leg[2])
                b, target = routes.received(h, full), routes.neighbour(h, full, -1)
                each_cut(b, lambda c: copy(h, full, b, target, c).start())
                started.append((h, full, b, target))

    def absorb(*leg):
        for h in range(2):
            for d in (1, -1):
                full = (leg[0], leg[1], d, leg[2])
                b, target = routes.sent(h, full), routes.neighbour(h, full, -1)
                k = h * len(LEGS) + LEG_INDEX[full]

                def add(c):
                    copy(h, full, b, target, c).wait_recv()
                    cut = leg_cut(full, b, c)
                    update[h, b, cut] = update[h, b, cut] + landed[k, cut]

                each_cut(b, add)

    def compute(places):
        for dy, dz in places:
            adjoint_block(update, tables, weights, routes.block(0, dy, dz))

    compute([(2, 2)])
    send(1, 2, 1)
    compute([(1, 2), (-1, 2), (2, 1), (2, -1)])
    send(1, 1, 1)
    send(1, -1, 1)
    absorb(1, 2, 1)
    send(1, 2, 0)
    compute([(2, 0), (0, 2)])
    send(1, 0, 1)
    compute([(1, 1), (1, -1), (-1, 1), (-1, -1)])
    absorb(1, 1, 1)
    absorb(1, -1, 1)
    send(1, 1, 0)
    send(1, -1, 0)
    absorb(1, 2, 0)
    send(0, 0, 1)
    compute([(1, 0), (-1, 0), (0, 1), (0, -1)])
    absorb(1, 0, 1)
    send(1, 0, 0)
    absorb(1, 1, 0)
    absorb(1, -1, 0)
    absorb(0, 0, 1)
    send(0, 0, 0)
    compute([(0, 0)])
    absorb(1, 0, 0)
    absorb(0, 0, 0)
    b = routes.me
    for s in range(SLOTS):
        for h in range(2):
            lanes = slice(h * HALF, h * HALF + HALF)
            degrees = b * WIDTH + h * HALF + lane_iota((4, HALF))
            keep = degrees >= jnp.maximum(ids_ref[s], 2)
            refined[s, :, lanes] = jnp.where(keep, harm_ref[s, :, lanes] + update[h, b, s], 0.0)
    for h, full, b, target in started:
        each_cut(b, lambda c: copy(h, full, b, target, c).wait_send())


def adjoint_scatter(order_ids, legendre, harmonics, returned):
    legs = 2 * len(LEGS)
    vmem = pl.BlockSpec(memory_space=pltpu.VMEM)
    return pl.pallas_call(
        adjoint_scatter_kernel,
        out_shape=jax.ShapeDtypeStruct(harmonics.shape, F32),
        in_specs=[
            pl.BlockSpec(memory_space=pltpu.SMEM),
            pl.BlockSpec(memory_space=pl.ANY),
            vmem,
            vmem,
        ],
        out_specs=vmem,
        scratch_shapes=[
            pltpu.VMEM(legendre.shape, F32),
            pltpu.VMEM((2, BLOCKS, SLOTS, 4, HALF), F32),
            pltpu.VMEM((legs, SLOTS, 4, HALF), F32),
            pltpu.VMEM((SLOTS, 8, 8, LANES), F32),
            pltpu.SemaphoreType.DMA((SLOTS,)),
            pltpu.SemaphoreType.DMA((legs * CUTS,)),
            pltpu.SemaphoreType.DMA((legs * CUTS,)),
        ],
        compiler_params=pltpu.CompilerParams(
            collective_id=2, has_side_effects=True, vmem_limit_bytes=VMEM_LIMIT
        ),
        name="adjoint_scatter",
    )(order_ids, legendre, harmonics, returned)


def to_rows(sky):
    cycles = sky.shape[0]
    parts = sky.reshape(cycles, 2, LANES, LANES)
    return jnp.transpose(parts, (0, 2, 1, 3)).reshape(cycles, 2 * LANES, LANES)


def from_rows(rows):
    cycles = rows.shape[0]
    parts = rows.reshape(cycles, LANES, 2, LANES)
    return jnp.transpose(parts, (0, 2, 1, 3)).reshape(cycles, 2, LANES * LANES)


def body(harmonics, legendre, sky_map, cycle_length, cycle_offset, cycle_weight, order_ids):
    scale = math.sqrt(8192 * 128 / 4194304)
    message = gather_forward(order_ids, legendre, harmonics)
    rows, returned = pixel_phase(
        scale, cycle_length, cycle_offset, cycle_weight, message, to_rows(sky_map)
    )
    refined = adjoint_scatter(order_ids, legendre, harmonics, returned)
    return refined, from_rows(rows)


def solution(mesh):
    return jax.shard_map(
        body,
        mesh=mesh,
        in_specs=(
            P("order", None, "blk"),
            P("order", None, "blk", None),
            P(("blk", "order"), None, None),
            P(("blk", "order")),
            P(("blk", "order")),
            P(("blk", "order")),
            P("order"),
        ),
        out_specs=(P("order", None, "blk"), P(("blk", "order"), None, None)),
        check_vma=False,
    )
```
